512 devices in a mesh: ka: 64 (over z_lo, y, core), rows: 8 (over x, z_hi).
Axes of the slice: x: 4, y: 8, z: 8 (z_hi: 2, z_lo: 4; z = z_hi * 4 + z_lo), core: 2. Of those that a mesh axis runs over, the one named last changes fastest.
Arguments:
- amplitudes: float32 [256, 64, 2, 2, 256], P('rows', 'ka'), may hold values from -6 to 6
- conduction_values: float32 [2, 512, 64, 256], P(None, 'rows', 'ka'), may hold values from -0.375 to 0.375
- valence_values: float32 [2, 512, 64, 256], P(None, 'rows', 'ka'), may hold values from -0.375 to 0.375
- screened: float32 [2, 64, 512, 512], P(None, None, 'ka', 'rows'), may hold values from -0.024 to 0.024
- conduction_energy: float32 [256, 64], P('rows', 'ka'), may hold values from 0.5 to 1
- valence_energy: float32 [64, 256], P('ka'), may hold values from -0.5 to 0
- offset_table: int32 [64, 64], replicated, may hold values from 0 to 63, as said below
Outputs:
- applied_once: float32 [256, 64, 2, 2, 256], P('rows', 'ka')
- applied_twice: float32 [256, 64, 2, 2, 256], P('rows', 'ka')
The draws below stay inside these ranges and needn't reach their ends.
Inputs may be any that keep to these rules, and one draw needn't show every extreme that they name: offset_table[k, k2] = 4 * 4 * a + 4 * b + d, where (a, b, d) are the coordinates of the grid point of k-point k minus those of k-point k2, each modulo 4, for a one to one assignment of the 64 k-points to the points of a 4 x 4 x 4 grid.
All inputs are finite; a program needn't handle non-finite values.
Results may differ from the reference program's by a relative error of at most 0.0003.
Values sent between devices are 32-bit elements; how exact they have to be, the bound alone decides.
No kernel may reach another device: no remote copies, remote signals or barrier semaphores. Data moves between devices by JAX's collectives and lax.ppermute only.
A program may use at most 64 MiB of HBM per device.

```python
import math
import jax
import jax.numpy as jnp
from jax import lax

KG = 4
K = 64
NMU = 512
C = 256
V = 256
NVEC = 2


def draw_offset_table(key, part):
    placed = jax.random.permutation(jax.random.fold_in(key, 11), K).astype(jnp.int32)
    first_axis = placed // (KG * KG)
    second_axis = placed // KG % KG
    third_axis = placed % KG
    first_diff = (first_axis[:, None] - first_axis[None, :]) % KG
    second_diff = (second_axis[:, None] - second_axis[None, :]) % KG
    third_diff = (third_axis[:, None] - third_axis[None, :]) % KG
    return (first_diff * KG * KG + second_diff * KG + third_diff).astype(jnp.int32)


def steps_of(own_key, shape, split, low, high):
    factor_of = 1.0
    for position, parts in split:
        draws = jax.random.uniform(jax.random.fold_in(jax.random.fold_in(own_key, 6), position), (parts,), jnp.float32, low / len(split), high / len(split))
        factor_of = factor_of * jnp.repeat(jnp.exp(draws), shape[position] // parts).reshape((-1,) + (1,) * (len(shape) - 1 - position))
    return factor_of


def centred(stream_key, dims, width, bound, pieces=(), kind=jnp.bfloat16):
    level = steps_of(stream_key, dims, pieces, -0.22, 0.18) if pieces else 1.0
    array = jax.random.normal(stream_key, dims, jnp.float32) * width * level
    return jnp.minimum(jnp.maximum(array, -bound), bound).astype(kind)


def setup_inputs(seed: int = 0) -> dict:
    arg_keys = jax.random.split(jax.random.key(seed), 8)
    return {
        "amplitudes": centred(arg_keys[0], (C, K, 2, NVEC, V), 1.0, 6.0, ((0, 8), (1, 64)), jnp.float32),
        "conduction_values": centred(arg_keys[1], (2, NMU, K, C), 0.0625, 0.375, ((1, 8), (2, 64)), jnp.float32),
        "valence_values": centred(arg_keys[2], (2, NMU, K, V), 0.0625, 0.375, ((1, 8), (2, 64)), jnp.float32),
        "screened": centred(arg_keys[3], (2, K, NMU, NMU), 0.004, 0.024, ((2, 64), (3, 8)), jnp.float32),
        "conduction_energy": jnp.clip(0.5 + 0.5 * jax.random.uniform(arg_keys[4], (C, K), jnp.float32) ** steps_of(arg_keys[4], (C, K), ((0, 8), (1, 64)), -0.2, 0.2), 0.5, 1.0),
        "valence_energy": jnp.clip(-0.5 + 0.5 * jax.random.uniform(arg_keys[5], (K, V), jnp.float32) ** steps_of(arg_keys[5], (K, V), ((0, 64),), -0.2, 0.2), -0.5, 0.0),
        "offset_table": draw_offset_table(jax.random.fold_in(arg_keys[7], 71), 0),
    }


def product(formula, left, right):
    return jnp.einsum(formula, left, right, precision=lax.Precision.HIGHEST)


def complex_multiply(formula, left_pair, right_pair):
    real_part = product(formula, left_pair[0], right_pair[0]) - product(formula, left_pair[1], right_pair[1])
    imag_part = product(formula, left_pair[0], right_pair[1]) + product(formula, left_pair[1], right_pair[0])
    return real_part, imag_part


def conjugated_rows(pair):
    return pair[0], -pair[1]


def decode(flat, grid_side):
    return jnp.stack([flat // (grid_side * grid_side), (flat // grid_side) % grid_side, flat % grid_side], axis=0)


def phase_table(left_flat, right_flat, grid_side):
    turns = jnp.sum(decode(left_flat, grid_side)[:, :, None] * decode(right_flat, grid_side)[:, None, :], axis=0) % grid_side
    angle = turns.astype(jnp.float32) * (2.0 * math.pi / grid_side)
    return jnp.cos(angle), -jnp.sin(angle)


def spectral(kernel_block, weight_pair, forward):
    moments = complex_multiply("rk,sknm->srnm", forward, (kernel_block[0], kernel_block[1]))
    scaled_real = weight_pair[0][None] * moments[0] - weight_pair[1][None] * moments[1]
    scaled_imag = weight_pair[0][None] * moments[1] + weight_pair[1][None] * moments[0]
    result = complex_multiply("rk,srnm->sknm", conjugated_rows(forward), (scaled_real, scaled_imag))
    return jnp.stack(result, axis=0) / forward[0].shape[0]


def reference(amplitudes, conduction_values, valence_values, screened, conduction_energy, valence_energy, offset_table):
    frequencies = jnp.arange(K, dtype=jnp.int32)
    forward = phase_table(frequencies, offset_table[:, 0].astype(jnp.int32), KG)
    forward_grid = phase_table(frequencies, frequencies, KG)
    valence_couple = (valence_values[0], valence_values[1])
    energy = (conduction_energy[:, :, None] - valence_energy[None])[:, :, None, None, :]
    kernel_block = min(NMU, 128)
    block_count = NMU // kernel_block

    def apply(state):
        state_pair = (state[:, :, 0], state[:, :, 1])

        def step(carry, block_index):
            start = (block_index * kernel_block).astype(jnp.int32)
            cond_block = tuple(lax.dynamic_slice_in_dim(part, start, kernel_block, 0) for part in (conduction_values[0], conduction_values[1]))
            weight_block = tuple(lax.dynamic_slice_in_dim(part, start, kernel_block, 2) for part in (screened[0], screened[1]))
            weights = complex_multiply("rq,qnm->rnm", forward_grid, weight_block)
            mixed_orbitals = complex_multiply("mkc,cksv->skmv", cond_block, state_pair)
            orbital_pairs = complex_multiply("zudg,cug->zucd", mixed_orbitals, conjugated_rows(valence_couple))
            convolution_result = spectral(jnp.stack(orbital_pairs, axis=0), weights, forward)
            summed_terms = complex_multiply("bxra,rxo->bxao", (convolution_result[0], convolution_result[1]), valence_couple)
            term = complex_multiply("mkc,skmv->cksv", conjugated_rows(cond_block), summed_terms)
            return (carry[0] + term[0], carry[1] + term[1]), None

        zeros = jnp.zeros(state_pair[0].shape, jnp.float32)
        total, unused = lax.scan(step, (zeros, zeros), jnp.arange(block_count, dtype=jnp.int32))
        return energy * state + jnp.stack(total, axis=2)

    first = apply(amplitudes)
    return first, apply(first)
```

```python
import jax
import jax.numpy as jnp
from jax import lax
from jax.experimental import pallas as pl
from jax.experimental.pallas import tpu as pltpu
from jax.sharding import Mesh, PartitionSpec as P


KA = ("zl", "y", "core")
ROWS = ("x", "zh")
F32, BF16 = jnp.float32, jnp.bfloat16
VMEM = pl.BlockSpec(memory_space=pltpu.VMEM)
SMEM = pl.BlockSpec(memory_space=pltpu.SMEM)

PARAMS = pltpu.CompilerParams(vmem_limit_bytes=20 * 2**20)

NN = (((1,), (0,)), ((), ()))
NT = (((1,), (1,)), ((), ()))


def shape(dims, dtype=F32):
    return jax.ShapeDtypeStruct(dims, dtype)


def split(value):
    high = value.astype(BF16)
    return high, (value - high.astype(F32)).astype(BF16)


def dot3(left, right, dims):
    def one(a, b):
        return lax.dot_general(a, b, dims, preferred_element_type=F32)

    return one(left[0], right[0]) + (one(left[0], right[1]) + one(left[1], right[0]))


def complex_pair(real, imag):
    return jnp.concatenate(
        [jnp.concatenate([real, imag], axis=1), jnp.concatenate([-imag, real], axis=1)], axis=0
    )


def with_turned(mixed):
    half = mixed.shape[1] // 2
    turned = jnp.concatenate([mixed[:, half:], -mixed[:, :half]], axis=1)
    return split(jnp.concatenate([mixed, turned], axis=0))


def transposed(ref):
    half = ref.shape[1] // 2
    return jnp.concatenate([ref[:, :half].T, ref[:, half:].T], axis=1)


def multiply_out(real, imag, pc_h, pc_l, qc_h, qc_l, out):
    mixed = dot3((pc_h[...], pc_l[...]), split(complex_pair(real, imag)), NN)
    pairs = dot3((qc_h[...], qc_l[...]), with_turned(mixed), NT)
    out[:, 0:8, :] = pairs[:, :128].reshape(64, 8, 128)
    out[:, 8:16, :] = pairs[:, 128:].reshape(64, 8, 128)


def first_kernel(zh, own, par, p_own, p_par, pc_h, pc_l, qc_h, qc_l, out):
    mine = zh[0]
    real, imag = [], []
    for x in range(4):
        for h in range(2):
            rows = pl.ds((2 * x + h) * 64, 64)
            for part in range(2):
                source = pl.ds(part * 64, 64)
                piece = jnp.where(mine == h, own[x, source, :], par[x, source, :])
                high, low = split(piece)
                qc_h[rows, pl.ds(part * 256, 256)] = high
                qc_l[rows, pl.ds(part * 256, 256)] = low
                source = pl.ds(128 + part * 32, 32)
                piece = jnp.where(mine == h, own[x, source, :], par[x, source, :])
                (imag if part else real).append(piece)
    for h in range(2):
        for part in range(2):
            source = pl.ds(part * 64, 64)
            piece = jnp.where(mine == h, p_own[source, :], p_par[source, :])
            high, low = split(piece)
            pc_h[pl.ds(h * 64, 64), pl.ds(part * 256, 256)] = high
            pc_l[pl.ds(h * 64, 64), pl.ds(part * 256, 256)] = low
    real, imag = jnp.concatenate(real, axis=0), jnp.concatenate(imag, axis=0)
    multiply_out(real, imag, pc_h, pc_l, qc_h, qc_l, out)


def first(zh, own, par, p_own, p_par):
    return pl.pallas_call(
        first_kernel,
        out_shape=(
            shape((128, 512), BF16),
            shape((128, 512), BF16),
            shape((512, 512), BF16),
            shape((512, 512), BF16),
            shape((64, 16, 128)),
        ),
        in_specs=[SMEM] + [VMEM] * 4,
        out_specs=(VMEM,) * 5,
        name="first",
        compiler_params=PARAMS,
    )(zh, own, par, p_own, p_par)


def forward_kernel(state, pc_h, pc_l, qc_h, qc_l, out):
    real = jnp.concatenate([state[x, h, 0] for x in range(4) for h in range(2)], axis=0)
    imag = jnp.concatenate([state[x, h, 1] for x in range(4) for h in range(2)], axis=0)
    multiply_out(real, imag, pc_h, pc_l, qc_h, qc_l, out)


def forward(state, pc, qc):
    return pl.pallas_call(
        forward_kernel,
        out_shape=shape((64, 16, 128)),
        in_specs=[VMEM] * 5,
        out_specs=VMEM,
        name="forward",
        compiler_params=PARAMS,
    )(state, *pc, *qc)


def backward_kernel(block, pc_h, pc_l, qc_h, qc_l, out):
    real = block[:, 0:8, :].reshape(512, 128)
    imag = block[:, 8:16, :].reshape(512, 128)
    valence = (transposed(qc_h), transposed(qc_l))
    mixed = dot3(valence, split(complex_pair(real, imag)), NN)
    conduction = (transposed(pc_h), transposed(pc_l))
    term = dot3(conduction, with_turned(mixed), NT)
    for row in range(8):
        out[row, 0] = term[row * 32 : row * 32 + 32, :256]
        out[row, 1] = term[row * 32 : row * 32 + 32, 256:]


def backward(block, pc, qc):
    return pl.pallas_call(
        backward_kernel,
        out_shape=shape((8, 2, 32, 256)),
        in_specs=[VMEM] * 5,
        out_specs=VMEM,
        name="backward",
        compiler_params=PARAMS,
    )(block, *pc, *qc)


def once_kernel(zh, keep, got, out):
    mine = zh[0]
    for part in range(2):
        low = jnp.where(mine == 0, keep[part], got[part])
        high = jnp.where(mine == 0, got[part], keep[part])
        out[:, 0, part] = jnp.stack([low, high], axis=1)


def place_once(zh, keep, got):
    return pl.pallas_call(
        once_kernel,
        out_shape=shape((32, 1, 2, 2, 256)),
        in_specs=[SMEM, VMEM, VMEM],
        out_specs=VMEM,
        name="place_once",
        compiler_params=PARAMS,
    )(zh, keep, got)


def twice_kernel(once, energy, parts, out):
    for part in range(2):
        terms = []
        for vector in range(2):
            rows = [parts[2 * x + vector, pl.ds(32 * part, 32), :] for x in range(4)]
            terms.append((rows[0] + rows[1]) + (rows[2] + rows[3]))
        factor = energy[...]
        factor = jnp.stack([factor, factor], axis=1)
        out[:, 0, part] = factor * once[:, 0, part] + jnp.stack(terms, axis=1)


def place_twice(once, energy, parts):
    return pl.pallas_call(
        twice_kernel,
        out_shape=shape((32, 1, 2, 2, 256)),
        in_specs=[VMEM] * 3,
        out_specs=VMEM,
        name="place_twice",
        compiler_params=PARAMS,
    )(once, energy, parts)


def butterfly(values, sign):
    (r0, i0), (r1, i1), (r2, i2), (r3, i3) = values
    ar, ai, br, bi = r0 + r2, i0 + i2, r0 - r2, i0 - i2
    cr, ci, dr, di = r1 + r3, i1 + i3, r1 - r3, i1 - i3
    plus, minus = (br - di, bi + dr), (br + di, bi - dr)
    first, last = (minus, plus) if sign < 0 else (plus, minus)
    return [(ar + cr, ai + ci), first, (ar - cr, ai - ci), last]


def plane(values, sign):
    for row in range(4):
        values[4 * row : 4 * row + 4] = butterfly(values[4 * row : 4 * row + 4], sign)
    for column in range(4):
        values[column::4] = butterfly(values[column::4], sign)
    return values


def read(ref, index):
    return ref[index, 0:8, :], ref[index, 8:16, :]


def write(ref, index, value):
    ref[index, 0:8, :], ref[index, 8:16, :] = value


def weights_kernel(zh, own, par, out):
    mine = zh[0]
    lane = lax.broadcasted_iota(jnp.int32, (8, 128), 1)
    for a in range(4):
        values = []
        for f in range(16 * a, 16 * a + 16):
            rows = pl.ds(f % 32 * 8, 8)
            columns = pl.ds(f // 32 * 128, 128)
            there = par[pl.ds(128 + f % 32 * 8, 8), columns]
            here = own[rows, columns]
            low = jnp.where(mine == 0, here, there)
            high = jnp.where(mine == 0, there, here)
            real = jnp.where(lane < 64, low, pltpu.roll(high, 64, 1)) * (1.0 / 64)
            imag = jnp.where(lane < 64, pltpu.roll(low, 64, 1), high) * (1.0 / 64)
            values.append((real, imag))
        for f, value in enumerate(plane(values, -1)):
            write(out, 16 * a + f, value)
    for f in range(16):
        values = butterfly([read(out, 16 * a + f) for a in range(4)], -1)
        for a in range(4):
            write(out, 16 * a + f, values[a])


def transform_weights(zh, own, par):
    return pl.pallas_call(
        weights_kernel,
        out_shape=shape((64, 16, 128)),
        in_specs=[SMEM, VMEM, VMEM],
        out_specs=VMEM,
        name="weights",
        compiler_params=PARAMS,
    )(zh, own, par)


def spectral_kernel(place, block, weight, out, work):
    for a in range(4):
        values = [read(block, place[16 * a + f]) for f in range(16)]
        for f, value in enumerate(plane(values, -1)):
            write(work, 16 * a + f, value)
    for f in range(16):
        values = butterfly([read(work, 16 * a + f) for a in range(4)], -1)
        scaled = []
        for a in range(4):
            (r, i), (wr, wi) = values[a], read(weight, 16 * a + f)
            scaled.append((wr * r - wi * i, wr * i + wi * r))
        values = butterfly(scaled, 1)
        for a in range(4):
            write(work, 16 * a + f, values[a])
    for a in range(4):
        values = plane([read(work, 16 * a + f) for f in range(16)], 1)
        for f in range(16):
            write(out, place[16 * a + f], values[f])


def spectral(place, block, weight):
    return pl.pallas_call(
        spectral_kernel,
        out_shape=shape((64, 16, 128)),
        in_specs=[SMEM, VMEM, VMEM],
        out_specs=VMEM,
        scratch_shapes=[pltpu.VMEM((64, 16, 128), F32)],
        name="spectral",
        compiler_params=PARAMS,
    )(place, block, weight)


def exchange(value, axes):
    return lax.all_to_all(value, axes, split_axis=0, concat_axis=0, tiled=True)


def gather_x(value):
    return exchange(jnp.broadcast_to(value[None], (4,) + value.shape), "x")


def swap(value):
    return lax.ppermute(value, "zh", [(0, 1), (1, 0)])


def per_device(
    amplitudes,
    conduction_values,
    valence_values,
    screened,
    conduction_energy,
    valence_energy,
    offset_table,
):
    zh = lax.axis_index("zh").astype(jnp.int32)
    first_half = zh == 0
    zh_scalar = zh[None]

    grid = offset_table[:, 0]
    points = jnp.arange(64, dtype=jnp.int32)
    place = jnp.sum(jnp.where(grid[None, :] == points[:, None], points[None, :], 0), axis=1)

    state = amplitudes[:, 0]
    s0 = state[:, :, 0].transpose(1, 0, 2).reshape(64, 256)
    s1 = state[:, :, 1].transpose(1, 0, 2).reshape(64, 256)
    keep = jnp.where(first_half, s0, s1)
    give = jnp.where(first_half, s1, s0)
    cond_row = jnp.pad(conduction_energy.reshape(1, 32), ((0, 7), (0, 224)))
    q_own = valence_values.reshape(128, 256)
    p_own = conduction_values.reshape(128, 256)
    par1 = swap(jnp.concatenate([q_own, give, cond_row], axis=0))
    w_own = jnp.concatenate(
        [screened[part, 32 * at : 32 * at + 32] for at in range(2) for part in range(2)], axis=-1
    ).reshape(256, 256)
    par2 = swap(jnp.concatenate([p_own, w_own], axis=0))

    own4 = gather_x(jnp.concatenate([q_own, keep], axis=0))
    par4 = gather_x(par1[:192])

    def ordered(own, par, axis):
        return jnp.where(
            first_half, jnp.stack([own, par], axis=axis), jnp.stack([par, own], axis=axis)
        )

    own_cond = conduction_energy[:, 0]
    par_cond = par1[192, :32]
    energy = (ordered(own_cond, par_cond, 0)[:, :, None] - valence_energy[0][None, None])[:, None]
    own_energy = own_cond[:, None] - valence_energy[0][None]
    state_q = ordered(keep.reshape(2, 32, 256), par1[128:192].reshape(2, 32, 256), 0)

    weight = transform_weights(zh_scalar, w_own, par2)
    own4, par4, weight, place, energy, own_energy, state_q = lax.optimization_barrier(
        (own4, par4, weight, place, energy, own_energy, state_q)
    )
    pc_h, pc_l, qc_h, qc_l, pairs = first(zh_scalar, own4, par4, p_own, par2)
    pc, qc = (pc_h, pc_l), (qc_h, qc_l)

    def convolve(block):
        sent = exchange(block, KA)
        back = exchange(spectral(place, sent, weight), KA)
        return backward(back, pc, qc)

    parts = exchange(convolve(pairs).reshape(4, 128, 256), "x")
    parts = parts.reshape(4, 2, 2, 32, 256)
    state_q = energy * state_q + jnp.sum(parts, axis=0)
    state_all = gather_x(state_q)

    keep = jnp.where(first_half, state_q[0], state_q[1])
    give = jnp.where(first_half, state_q[1], state_q[0])
    got = swap(give.reshape(64, 256)).reshape(2, 32, 256)
    once = place_once(zh_scalar, keep, got)

    pairs = forward(state_all, pc, qc)
    parts = exchange(convolve(pairs).reshape(8, 64, 256), ROWS)
    return once, place_twice(once, own_energy, parts)


def solution(mesh):
    fine = Mesh(mesh.devices.reshape(4, 8, 2, 4, 2), KA + ROWS)
    specs = (
        P(ROWS, KA, None, None, None),
        P(None, ROWS, KA, None),
        P(None, ROWS, KA, None),
        P(None, None, KA, ROWS),
        P(ROWS, KA),
        P(KA, None),
        P(),
    )

    return jax.shard_map(
        per_device,
        mesh=fine,
        in_specs=specs,
        out_specs=(P(ROWS, KA, None, None, None),) * 2,
        check_vma=False,
    )
```

```python
import jax
import jax.numpy as jnp
from jax import lax
from jax.experimental import pallas as pl
from jax.experimental.pallas import tpu as pltpu
from jax.sharding import Mesh, PartitionSpec as P


KA = ("zl", "y", "core")
ROWS = ("x", "zh")
F32, BF16 = jnp.float32, jnp.bfloat16
VMEM = pl.BlockSpec(memory_space=pltpu.VMEM)
SMEM = pl.BlockSpec(memory_space=pltpu.SMEM)

PARAMS = pltpu.CompilerParams(vmem_limit_bytes=20 * 2**20)

NN = (((1,), (0,)), ((), ()))
NT = (((1,), (1,)), ((), ()))


def shape(dims, dtype=F32):
    return jax.ShapeDtypeStruct(dims, dtype)


def split(value):
    high = value.astype(BF16)
    return high, (value - high.astype(F32)).astype(BF16)


def dot3(left, right, dims):
    def one(a, b):
        return lax.dot_general(a, b, dims, preferred_element_type=F32)

    return one(left[0], right[0]) + (one(left[0], right[1]) + one(left[1], right[0]))


def complex_pair(real, imag):
    return jnp.concatenate(
        [jnp.concatenate([real, imag], axis=1), jnp.concatenate([-imag, real], axis=1)], axis=0
    )


def with_turned(mixed):
    half = mixed.shape[1] // 2
    turned = jnp.concatenate([mixed[:, half:], -mixed[:, :half]], axis=1)
    return split(jnp.concatenate([mixed, turned], axis=0))


def transposed(ref):
    half = ref.shape[1] // 2
    return jnp.concatenate([ref[:, :half].T, ref[:, half:].T], axis=1)


def multiply_out(real, imag, pc_h, pc_l, qc_h, qc_l, out):
    mixed = dot3((pc_h[...], pc_l[...]), split(complex_pair(real, imag)), NN)
    pairs = dot3((qc_h[...], qc_l[...]), with_turned(mixed), NT)
    out[:, 0:8, :] = pairs[:, :128].reshape(64, 8, 128)
    out[:, 8:16, :] = pairs[:, 128:].reshape(64, 8, 128)


def first_kernel(zh, own, par, p_own, p_par, pc_h, pc_l, qc_h, qc_l, out):
    mine = zh[0]
    real, imag = [], []
    for x in range(4):
        for h in range(2):
            rows = pl.ds((2 * x + h) * 64, 64)
            for part in range(2):
                source = pl.ds(part * 64, 64)
                piece = jnp.where(mine == h, own[x, source, :], par[x, source, :])
                high, low = split(piece)
                qc_h[rows, pl.ds(part * 256, 256)] = high
                qc_l[rows, pl.ds(part * 256, 256)] = low
                source = pl.ds(128 + part * 32, 32)
                piece = jnp.where(mine == h, own[x, source, :], par[x, source, :])
                (imag if part else real).append(piece)
    for h in range(2):
        for part in range(2):
            source = pl.ds(part * 64, 64)
            piece = jnp.where(mine == h, p_own[source, :], p_par[source, :])
            high, low = split(piece)
            pc_h[pl.ds(h * 64, 64), pl.ds(part * 256, 256)] = high
            pc_l[pl.ds(h * 64, 64), pl.ds(part * 256, 256)] = low
    real, imag = jnp.concatenate(real, axis=0), jnp.concatenate(imag, axis=0)
    multiply_out(real, imag, pc_h, pc_l, qc_h, qc_l, out)


def first(zh, own, par, p_own, p_par):
    return pl.pallas_call(
        first_kernel,
        out_shape=(
            shape((128, 512), BF16),
            shape((128, 512), BF16),
            shape((512, 512), BF16),
            shape((512, 512), BF16),
            shape((64, 16, 128)),
        ),
        in_specs=[SMEM] + [VMEM] * 4,
        out_specs=(VMEM,) * 5,
        name="first",
        compiler_params=PARAMS,
    )(zh, own, par, p_own, p_par)


def forward_kernel(state, pc_h, pc_l, qc_h, qc_l, out):
    real = jnp.concatenate([state[x, h, 0] for x in range(4) for h in range(2)], axis=0)
    imag = jnp.concatenate([state[x, h, 1] for x in range(4) for h in range(2)], axis=0)
    multiply_out(real, imag, pc_h, pc_l, qc_h, qc_l, out)


def forward(state, pc, qc):
    return pl.pallas_call(
        forward_kernel,
        out_shape=shape((64, 16, 128)),
        in_specs=[VMEM] * 5,
        out_specs=VMEM,
        name="forward",
        compiler_params=PARAMS,
    )(state, *pc, *qc)


def backward_kernel(block, pc_h, pc_l, qc_h, qc_l, out):
    real = block[:, 0:8, :].reshape(512, 128)
    imag = block[:, 8:16, :].reshape(512, 128)
    valence = (transposed(qc_h), transposed(qc_l))
    mixed = dot3(valence, split(complex_pair(real, imag)), NN)
    conduction = (transposed(pc_h), transposed(pc_l))
    term = dot3(conduction, with_turned(mixed), NT)
    for row in range(8):
        out[row, 0] = term[row * 32 : row * 32 + 32, :256]
        out[row, 1] = term[row * 32 : row * 32 + 32, 256:]


def backward(block, pc, qc):
    return pl.pallas_call(
        backward_kernel,
        out_shape=shape((8, 2, 32, 256)),
        in_specs=[VMEM] * 5,
        out_specs=VMEM,
        name="backward",
        compiler_params=PARAMS,
    )(block, *pc, *qc)


def update_kernel(zh, state, energy, parts, out, keep, give):
    mine = zh[0]
    values = []
    for h in range(2):
        for part in range(2):
            rows = [parts[x, pl.ds(64 * h + 32 * part, 32), :] for x in range(4)]
            term = (rows[0] + rows[1]) + (rows[2] + rows[3])
            value = energy[h] * state[h, part] + term
            for x in range(4):
                out[x, h, part] = value
            values.append(value)
    for part in range(2):
        keep[part] = jnp.where(mine == 0, values[part], values[2 + part])
        give[pl.ds(32 * part, 32), :] = jnp.where(mine == 0, values[2 + part], values[part])


def update(zh, state, energy, parts):
    return pl.pallas_call(
        update_kernel,
        out_shape=(shape((4, 2, 2, 32, 256)), shape((2, 32, 256)), shape((64, 256))),
        in_specs=[SMEM] + [VMEM] * 3,
        out_specs=(VMEM,) * 3,
        name="update",
        compiler_params=PARAMS,
    )(zh, state, energy, parts)


def finish_kernel(zh, keep, got, energy, parts, once, twice):
    mine = zh[0]
    factor = energy[...]
    factor = jnp.stack([factor, factor], axis=1)
    for part in range(2):
        here, there = keep[part], got[pl.ds(32 * part, 32), :]
        low = jnp.where(mine == 0, here, there)
        high = jnp.where(mine == 0, there, here)
        before = jnp.stack([low, high], axis=1)
        terms = []
        for vector in range(2):
            rows = [parts[2 * x + vector, pl.ds(32 * part, 32), :] for x in range(4)]
            terms.append((rows[0] + rows[1]) + (rows[2] + rows[3]))
        once[:, 0, part] = before
        twice[:, 0, part] = factor * before + jnp.stack(terms, axis=1)


def finish(zh, keep, got, energy, parts):
    return pl.pallas_call(
        finish_kernel,
        out_shape=(shape((32, 1, 2, 2, 256)),) * 2,
        in_specs=[SMEM] + [VMEM] * 4,
        out_specs=(VMEM,) * 2,
        name="finish",
        compiler_params=PARAMS,
    )(zh, keep, got, energy, parts)


def butterfly(values, sign):
    (r0, i0), (r1, i1), (r2, i2), (r3, i3) = values
    ar, ai, br, bi = r0 + r2, i0 + i2, r0 - r2, i0 - i2
    cr, ci, dr, di = r1 + r3, i1 + i3, r1 - r3, i1 - i3
    plus, minus = (br - di, bi + dr), (br + di, bi - dr)
    first, last = (minus, plus) if sign < 0 else (plus, minus)
    return [(ar + cr, ai + ci), first, (ar - cr, ai - ci), last]


def plane(values, sign):
    for row in range(4):
        values[4 * row : 4 * row + 4] = butterfly(values[4 * row : 4 * row + 4], sign)
    for column in range(4):
        values[column::4] = butterfly(values[column::4], sign)
    return values


def read(ref, index):
    return ref[index, 0:8, :], ref[index, 8:16, :]


def write(ref, index, value):
    ref[index, 0:8, :], ref[index, 8:16, :] = value


def weights_kernel(zh, own, par, out):
    mine = zh[0]
    lane = lax.broadcasted_iota(jnp.int32, (8, 128), 1)
    for a in range(4):
        values = []
        for f in range(16 * a, 16 * a + 16):
            rows = pl.ds(f % 32 * 8, 8)
            columns = pl.ds(f // 32 * 128, 128)
            there = par[pl.ds(128 + f % 32 * 8, 8), columns]
            here = own[pl.ds(128 + f % 32 * 8, 8), columns]
            low = jnp.where(mine == 0, here, there)
            high = jnp.where(mine == 0, there, here)
            real = jnp.where(lane < 64, low, pltpu.roll(high, 64, 1)) * (1.0 / 64)
            imag = jnp.where(lane < 64, pltpu.roll(low, 64, 1), high) * (1.0 / 64)
            values.append((real, imag))
        for f, value in enumerate(plane(values, -1)):
            write(out, 16 * a + f, value)
    for f in range(16):
        values = butterfly([read(out, 16 * a + f) for a in range(4)], -1)
        for a in range(4):
            write(out, 16 * a + f, values[a])


def transform_weights(zh, own, par):
    return pl.pallas_call(
        weights_kernel,
        out_shape=shape((64, 16, 128)),
        in_specs=[SMEM, VMEM, VMEM],
        out_specs=VMEM,
        name="weights",
        compiler_params=PARAMS,
    )(zh, own, par)


def spectral_kernel(place, block, weight, out, work):
    for a in range(4):
        values = [read(block, place[16 * a + f]) for f in range(16)]
        for f, value in enumerate(plane(values, -1)):
            write(work, 16 * a + f, value)
    for f in range(16):
        values = butterfly([read(work, 16 * a + f) for a in range(4)], -1)
        scaled = []
        for a in range(4):
            (r, i), (wr, wi) = values[a], read(weight, 16 * a + f)
            scaled.append((wr * r - wi * i, wr * i + wi * r))
        values = butterfly(scaled, 1)
        for a in range(4):
            write(work, 16 * a + f, values[a])
    for a in range(4):
        values = plane([read(work, 16 * a + f) for f in range(16)], 1)
        for f in range(16):
            write(out, place[16 * a + f], values[f])


def spectral(place, block, weight):
    return pl.pallas_call(
        spectral_kernel,
        out_shape=shape((64, 16, 128)),
        in_specs=[SMEM, VMEM, VMEM],
        out_specs=VMEM,
        scratch_shapes=[pltpu.VMEM((64, 16, 128), F32)],
        name="spectral",
        compiler_params=PARAMS,
    )(place, block, weight)


def exchange(value, axes):
    return lax.all_to_all(value, axes, split_axis=0, concat_axis=0, tiled=True)


def gather_x(value):
    return exchange(jnp.broadcast_to(value[None], (4,) + value.shape), "x")


def swap(value):
    return lax.ppermute(value, "zh", [(0, 1), (1, 0)])


def per_device(
    amplitudes,
    conduction_values,
    valence_values,
    screened,
    conduction_energy,
    valence_energy,
    offset_table,
):
    zh = lax.axis_index("zh").astype(jnp.int32)
    first_half = zh == 0
    zh_scalar = zh[None]

    grid = offset_table[:, 0]
    points = jnp.arange(64, dtype=jnp.int32)
    place = jnp.sum(jnp.where(grid[None, :] == points[:, None], points[None, :], 0), axis=1)

    state = amplitudes[:, 0]
    s0 = state[:, :, 0].transpose(1, 0, 2).reshape(64, 256)
    s1 = state[:, :, 1].transpose(1, 0, 2).reshape(64, 256)
    keep = jnp.where(first_half, s0, s1)
    give = jnp.where(first_half, s1, s0)
    q_own = valence_values.reshape(128, 256)
    par1 = swap(jnp.concatenate([q_own, give], axis=0))

    cond_row = jnp.pad(conduction_energy.reshape(1, 32), ((0, 7), (0, 224)))
    w_own = jnp.concatenate(
        [screened[part, 32 * at : 32 * at + 32] for at in range(2) for part in range(2)], axis=-1
    ).reshape(256, 256)
    own2 = jnp.concatenate([conduction_values.reshape(128, 256), w_own, cond_row], axis=0)
    par2 = swap(own2)

    own4 = gather_x(jnp.concatenate([q_own, keep], axis=0))
    par4 = gather_x(par1)

    def ordered(own, par, axis):
        return jnp.where(
            first_half, jnp.stack([own, par], axis=axis), jnp.stack([par, own], axis=axis)
        )

    weight = transform_weights(zh_scalar, own2, par2)
    cond = ordered(own2[384, :32], par2[384, :32], 0)
    energy = cond[:, :, None] - valence_energy[0][None, None]
    own_energy = own2[384, :32][:, None] - valence_energy[0][None]
    state_q = ordered(keep.reshape(2, 32, 256), par1[128:].reshape(2, 32, 256), 0)
    own4, par4, weight, place, energy, own_energy, state_q = lax.optimization_barrier(
        (own4, par4, weight, place, energy, own_energy, state_q)
    )
    pc_h, pc_l, qc_h, qc_l, pairs = first(zh_scalar, own4, par4, own2, par2)
    pc, qc = (pc_h, pc_l), (qc_h, qc_l)

    def convolve(block):
        sent = exchange(block, KA)
        back = exchange(spectral(place, sent, weight), KA)
        return backward(back, pc, qc)

    parts = exchange(convolve(pairs).reshape(4, 128, 256), "x")
    state_four, keep, give = update(zh_scalar, state_q, energy, parts)
    got = swap(give)
    state_all = exchange(state_four, "x")

    pairs = forward(state_all, pc, qc)
    parts = exchange(convolve(pairs).reshape(8, 64, 256), ROWS)
    return finish(zh_scalar, keep, got, own_energy, parts)


def solution(mesh):
    fine = Mesh(mesh.devices.reshape(4, 8, 2, 4, 2), KA + ROWS)
    specs = (
        P(ROWS, KA, None, None, None),
        P(None, ROWS, KA, None),
        P(None, ROWS, KA, None),
        P(None, None, KA, ROWS),
        P(ROWS, KA),
        P(KA, None),
        P(),
    )

    return jax.shard_map(
        per_device,
        mesh=fine,
        in_specs=specs,
        out_specs=(P(ROWS, KA, None, None, None),) * 2,
        check_vma=False,
    )
```

```python
import jax
import jax.numpy as jnp
from jax import lax
from jax.experimental import pallas as pl
from jax.experimental.pallas import tpu as pltpu
from jax.sharding import Mesh, PartitionSpec as P


KA = ("zl", "y", "core")
ROWS = ("x", "zh")
F32, BF16 = jnp.float32, jnp.bfloat16
VMEM = pl.BlockSpec(memory_space=pltpu.VMEM)
SMEM = pl.BlockSpec(memory_space=pltpu.SMEM)

PARAMS = pltpu.CompilerParams(vmem_limit_bytes=20 * 2**20)

NN = (((1,), (0,)), ((), ()))
NT = (((1,), (1,)), ((), ()))


def shape(dims, dtype=F32):
    return jax.ShapeDtypeStruct(dims, dtype)


def split(value):
    high = value.astype(BF16)
    return high, (value - high.astype(F32)).astype(BF16)


def dot3(left, right, dims):
    def one(a, b):
        return lax.dot_general(a, b, dims, preferred_element_type=F32)

    return one(left[0], right[0]) + (one(left[0], right[1]) + one(left[1], right[0]))


def complex_pair(real, imag):
    return jnp.concatenate(
        [jnp.concatenate([real, imag], axis=1), jnp.concatenate([-imag, real], axis=1)], axis=0
    )


def with_turned(mixed):
    half = mixed.shape[1] // 2
    turned = jnp.concatenate([mixed[:, half:], -mixed[:, :half]], axis=1)
    return split(jnp.concatenate([mixed, turned], axis=0))


def transposed(ref):
    half = ref.shape[1] // 2
    return jnp.concatenate([ref[:, :half].T, ref[:, half:].T], axis=1)


def multiply_out(real, imag, pc_h, pc_l, qc_h, qc_l, out):
    mixed = dot3((pc_h[...], pc_l[...]), split(complex_pair(real, imag)), NN)
    pairs = dot3((qc_h[...], qc_l[...]), with_turned(mixed), NT)
    out[:, 0:8, :] = pairs[:, :128].reshape(64, 8, 128)
    out[:, 8:16, :] = pairs[:, 128:].reshape(64, 8, 128)


def first_kernel(zh, own, par, pc_h, pc_l, qc_h, qc_l, out):
    mine = zh[0]
    real, imag = [], []
    for x in range(4):
        for h in range(2):
            rows = pl.ds((2 * x + h) * 64, 64)
            for part in range(2):
                source = pl.ds(part * 64, 64)
                piece = jnp.where(mine == h, own[x, source, :], par[x, source, :])
                high, low = split(piece)
                qc_h[rows, pl.ds(part * 256, 256)] = high
                qc_l[rows, pl.ds(part * 256, 256)] = low
                source = pl.ds(128 + part * 32, 32)
                piece = jnp.where(mine == h, own[x, source, :], par[x, source, :])
                (imag if part else real).append(piece)
    real, imag = jnp.concatenate(real, axis=0), jnp.concatenate(imag, axis=0)
    multiply_out(real, imag, pc_h, pc_l, qc_h, qc_l, out)


def first(zh, own, par, pc):
    return pl.pallas_call(
        first_kernel,
        out_shape=(
            shape((512, 512), BF16),
            shape((512, 512), BF16),
            shape((64, 16, 128)),
        ),
        in_specs=[SMEM] + [VMEM] * 4,
        out_specs=(VMEM,) * 3,
        name="first",
        compiler_params=PARAMS,
    )(zh, own, par, *pc)


def forward_kernel(state, pc_h, pc_l, qc_h, qc_l, out):
    real = jnp.concatenate([state[x, h, 0] for x in range(4) for h in range(2)], axis=0)
    imag = jnp.concatenate([state[x, h, 1] for x in range(4) for h in range(2)], axis=0)
    multiply_out(real, imag, pc_h, pc_l, qc_h, qc_l, out)


def forward(state, pc, qc):
    return pl.pallas_call(
        forward_kernel,
        out_shape=shape((64, 16, 128)),
        in_specs=[VMEM] * 5,
        out_specs=VMEM,
        name="forward",
        compiler_params=PARAMS,
    )(state, *pc, *qc)


def second_term(block, pc_h, pc_l, qc_h, qc_l):
    real = block[:, 0:8, :].reshape(512, 128)
    imag = block[:, 8:16, :].reshape(512, 128)
    valence = (transposed(qc_h), transposed(qc_l))
    mixed = dot3(valence, split(complex_pair(real, imag)), NN)
    conduction = (transposed(pc_h), transposed(pc_l))
    return dot3(conduction, with_turned(mixed), NT)


def backward_kernel(block, pc_h, pc_l, qc_h, qc_l, out):
    term = second_term(block, pc_h, pc_l, qc_h, qc_l)
    for row in range(8):
        out[row, 0] = term[row * 32 : row * 32 + 32, :256]
        out[row, 1] = term[row * 32 : row * 32 + 32, 256:]


def backward(block, pc, qc):
    return pl.pallas_call(
        backward_kernel,
        out_shape=shape((8, 2, 32, 256)),
        in_specs=[VMEM] * 5,
        out_specs=VMEM,
        name="backward",
        compiler_params=PARAMS,
    )(block, *pc, *qc)


def backward_apart_kernel(zh, block, pc_h, pc_l, qc_h, qc_l, mine_out, other_out):
    mine = zh[0]
    term = second_term(block, pc_h, pc_l, qc_h, qc_l)
    for x in range(4):
        for part in range(2):
            columns = slice(256 * part, 256 * part + 256)
            low = term[64 * x : 64 * x + 32, columns]
            high = term[64 * x + 32 : 64 * x + 64, columns]
            mine_out[x, pl.ds(32 * part, 32), :] = jnp.where(mine == 0, low, high)
            other_out[x, pl.ds(32 * part, 32), :] = jnp.where(mine == 0, high, low)


def backward_apart(zh, block, pc, qc):
    return pl.pallas_call(
        backward_apart_kernel,
        out_shape=(shape((4, 64, 256)),) * 2,
        in_specs=[SMEM] + [VMEM] * 5,
        out_specs=(VMEM,) * 2,
        name="backward_apart",
        compiler_params=PARAMS,
    )(zh, block, *pc, *qc)


def update_kernel(zh, state, energy, parts, out, keep, give):
    mine = zh[0]
    values = []
    for h in range(2):
        for part in range(2):
            rows = [parts[x, pl.ds(64 * h + 32 * part, 32), :] for x in range(4)]
            term = (rows[0] + rows[1]) + (rows[2] + rows[3])
            value = energy[h] * state[h, part] + term
            for x in range(4):
                out[x, h, part] = value
            values.append(value)
    for part in range(2):
        keep[part] = jnp.where(mine == 0, values[part], values[2 + part])
        give[pl.ds(32 * part, 32), :] = jnp.where(mine == 0, values[2 + part], values[part])


def update(zh, state, energy, parts):
    return pl.pallas_call(
        update_kernel,
        out_shape=(shape((4, 2, 2, 32, 256)), shape((2, 32, 256)), shape((64, 256))),
        in_specs=[SMEM] + [VMEM] * 3,
        out_specs=(VMEM,) * 3,
        name="update",
        compiler_params=PARAMS,
    )(zh, state, energy, parts)


def total(parts, rows):
    return (parts[0, rows, :] + parts[1, rows, :]) + (parts[2, rows, :] + parts[3, rows, :])


def other_half_kernel(zh, energy, give, parts, out):
    factor = jnp.where(zh[0] == 0, energy[1], energy[0])
    for part in range(2):
        rows = pl.ds(32 * part, 32)
        out[rows, :] = factor * give[rows, :] + total(parts, rows)


def other_half(zh, energy, give, parts):
    return pl.pallas_call(
        other_half_kernel,
        out_shape=shape((64, 256)),
        in_specs=[SMEM] + [VMEM] * 3,
        out_specs=VMEM,
        name="other_half",
        compiler_params=PARAMS,
    )(zh, energy, give, parts)


def finish_kernel(zh, keep, got, energy, parts, got_twice, once, twice):
    mine = zh[0]
    factor = jnp.where(mine == 0, energy[0], energy[1])

    def both(here, there):
        low, high = jnp.where(mine == 0, here, there), jnp.where(mine == 0, there, here)
        return jnp.stack([low, high], axis=1)

    for part in range(2):
        rows = pl.ds(32 * part, 32)
        once[:, 0, part] = both(keep[part], got[rows, :])
        own = factor * keep[part] + total(parts, rows)
        twice[:, 0, part] = both(own, got_twice[rows, :])


def finish(zh, keep, got, energy, parts, got_twice):
    return pl.pallas_call(
        finish_kernel,
        out_shape=(shape((32, 1, 2, 2, 256)),) * 2,
        in_specs=[SMEM] + [VMEM] * 5,
        out_specs=(VMEM,) * 2,
        name="finish",
        compiler_params=PARAMS,
    )(zh, keep, got, energy, parts, got_twice)


def butterfly(values, sign):
    (r0, i0), (r1, i1), (r2, i2), (r3, i3) = values
    ar, ai, br, bi = r0 + r2, i0 + i2, r0 - r2, i0 - i2
    cr, ci, dr, di = r1 + r3, i1 + i3, r1 - r3, i1 - i3
    plus, minus = (br - di, bi + dr), (br + di, bi - dr)
    first, last = (minus, plus) if sign < 0 else (plus, minus)
    return [(ar + cr, ai + ci), first, (ar - cr, ai - ci), last]


def plane(values, sign):
    for row in range(4):
        values[4 * row : 4 * row + 4] = butterfly(values[4 * row : 4 * row + 4], sign)
    for column in range(4):
        values[column::4] = butterfly(values[column::4], sign)
    return values


def read(ref, index):
    return ref[index, 0:8, :], ref[index, 8:16, :]


def write(ref, index, value):
    ref[index, 0:8, :], ref[index, 8:16, :] = value


def weights_kernel(zh, own, par, out, pc_h, pc_l):
    mine = zh[0]
    for h in range(2):
        for part in range(2):
            source = pl.ds(part * 64, 64)
            piece = jnp.where(mine == h, own[source, :], par[source, :])
            high, low = split(piece)
            pc_h[pl.ds(h * 64, 64), pl.ds(part * 256, 256)] = high
            pc_l[pl.ds(h * 64, 64), pl.ds(part * 256, 256)] = low
    lane = lax.broadcasted_iota(jnp.int32, (8, 128), 1)
    for a in range(4):
        values = []
        for f in range(16 * a, 16 * a + 16):
            rows = pl.ds(f % 32 * 8, 8)
            columns = pl.ds(f // 32 * 128, 128)
            there = par[pl.ds(128 + f % 32 * 8, 8), columns]
            here = own[pl.ds(128 + f % 32 * 8, 8), columns]
            low = jnp.where(mine == 0, here, there)
            high = jnp.where(mine == 0, there, here)
            real = jnp.where(lane < 64, low, pltpu.roll(high, 64, 1)) * (1.0 / 64)
            imag = jnp.where(lane < 64, pltpu.roll(low, 64, 1), high) * (1.0 / 64)
            values.append((real, imag))
        for f, value in enumerate(plane(values, -1)):
            write(out, 16 * a + f, value)
    for f in range(16):
        values = butterfly([read(out, 16 * a + f) for a in range(4)], -1)
        for a in range(4):
            write(out, 16 * a + f, values[a])


def transform_weights(zh, own, par):
    return pl.pallas_call(
        weights_kernel,
        out_shape=(shape((64, 16, 128)), shape((128, 512), BF16), shape((128, 512), BF16)),
        in_specs=[SMEM, VMEM, VMEM],
        out_specs=(VMEM,) * 3,
        name="weights",
        compiler_params=PARAMS,
    )(zh, own, par)


def spectral_kernel(place, block, weight, out, work):
    for a in range(4):
        values = [read(block, place[16 * a + f]) for f in range(16)]
        for f, value in enumerate(plane(values, -1)):
            write(work, 16 * a + f, value)
    for f in range(16):
        values = butterfly([read(work, 16 * a + f) for a in range(4)], -1)
        scaled = []
        for a in range(4):
            (r, i), (wr, wi) = values[a], read(weight, 16 * a + f)
            scaled.append((wr * r - wi * i, wr * i + wi * r))
        values = butterfly(scaled, 1)
        for a in range(4):
            write(work, 16 * a + f, values[a])
    for a in range(4):
        values = plane([read(work, 16 * a + f) for f in range(16)], 1)
        for f in range(16):
            write(out, place[16 * a + f], values[f])


def spectral(place, block, weight):
    return pl.pallas_call(
        spectral_kernel,
        out_shape=shape((64, 16, 128)),
        in_specs=[SMEM, VMEM, VMEM],
        out_specs=VMEM,
        scratch_shapes=[pltpu.VMEM((64, 16, 128), F32)],
        name="spectral",
        compiler_params=PARAMS,
    )(place, block, weight)


def exchange(value, axes):
    return lax.all_to_all(value, axes, split_axis=0, concat_axis=0, tiled=True)


def gather_x(value):
    return exchange(jnp.broadcast_to(value[None], (4,) + value.shape), "x")


def swap(value):
    return lax.ppermute(value, "zh", [(0, 1), (1, 0)])


def per_device(
    amplitudes,
    conduction_values,
    valence_values,
    screened,
    conduction_energy,
    valence_energy,
    offset_table,
):
    zh = lax.axis_index("zh").astype(jnp.int32)
    first_half = zh == 0
    zh_scalar = zh[None]

    grid = offset_table[:, 0]
    points = jnp.arange(64, dtype=jnp.int32)
    place = jnp.sum(jnp.where(grid[None, :] == points[:, None], points[None, :], 0), axis=1)

    state = amplitudes[:, 0]
    s0 = state[:, :, 0].transpose(1, 0, 2).reshape(64, 256)
    s1 = state[:, :, 1].transpose(1, 0, 2).reshape(64, 256)
    keep = jnp.where(first_half, s0, s1)
    give = jnp.where(first_half, s1, s0)
    q_own = valence_values.reshape(128, 256)
    par1 = swap(jnp.concatenate([q_own, give], axis=0))

    cond_row = jnp.pad(conduction_energy.reshape(1, 32), ((0, 7), (0, 224)))
    w_own = jnp.concatenate(
        [screened[part, 32 * at : 32 * at + 32] for at in range(2) for part in range(2)], axis=-1
    ).reshape(256, 256)
    own2 = jnp.concatenate([conduction_values.reshape(128, 256), w_own, cond_row], axis=0)
    par2 = swap(own2)

    own4 = gather_x(jnp.concatenate([q_own, keep], axis=0))
    par4 = gather_x(par1)

    def ordered(own, par, axis):
        return jnp.where(
            first_half, jnp.stack([own, par], axis=axis), jnp.stack([par, own], axis=axis)
        )

    weight, pc_h, pc_l = transform_weights(zh_scalar, own2, par2)
    cond = ordered(own2[384, :32], par2[384, :32], 0)
    energy = cond[:, :, None] - valence_energy[0][None, None]
    state_q = ordered(keep.reshape(2, 32, 256), par1[128:].reshape(2, 32, 256), 0)
    own4, par4, weight, pc_h, pc_l, place, energy, state_q = lax.optimization_barrier(
        (own4, par4, weight, pc_h, pc_l, place, energy, state_q)
    )
    pc = (pc_h, pc_l)
    qc_h, qc_l, pairs = first(zh_scalar, own4, par4, pc)
    qc = (qc_h, qc_l)

    def convolve(block):
        sent = exchange(block, KA)
        return exchange(spectral(place, sent, weight), KA)

    term = backward(convolve(pairs), pc, qc)
    parts = exchange(term.reshape(4, 128, 256), "x")
    state_four, keep, give = update(zh_scalar, state_q, energy, parts)
    got = swap(give)
    state_all = exchange(state_four, "x")

    back = convolve(forward(state_all, pc, qc))
    mine, other = backward_apart(zh_scalar, back, pc, qc)
    other = exchange(other, "x")
    got_twice = swap(other_half(zh_scalar, energy, give, other))
    mine = exchange(mine, "x")
    return finish(zh_scalar, keep, got, energy, mine, got_twice)


def solution(mesh):
    fine = Mesh(mesh.devices.reshape(4, 8, 2, 4, 2), KA + ROWS)
    specs = (
        P(ROWS, KA, None, None, None),
        P(None, ROWS, KA, None),
        P(None, ROWS, KA, None),
        P(None, None, KA, ROWS),
        P(ROWS, KA),
        P(KA, None),
        P(),
    )

    return jax.shard_map(
        per_device,
        mesh=fine,
        in_specs=specs,
        out_specs=(P(ROWS, KA, None, None, None),) * 2,
        check_vma=False,
    )
```
